32 devices in a mesh: section: 2 (over x), dp: 4 (over z), expert: 4 (over y, core).
Axes of the slice: x: 2, y: 2, z: 4, core: 2. Of those that a mesh axis runs over, the one named last changes fastest.
Arguments:
- cotangent: bfloat16 [2, 128, 2048], P('section', ('dp', 'expert')), may hold values from -6 to 6
- routes: int32 [2, 1, 128, 8], P('section', None, ('dp', 'expert')), may hold values from 0 to 15, as said below
- probs: float32 [2, 1, 128, 8], P('section', None, ('dp', 'expert')), may hold values from 0.1 to 0.5
- stash: bfloat16 [2, 1, 4, 4, 4, 4, 8, 1536], P('section', None, 'dp', 'expert'), may hold values from -6 to 6
- w_gate: bfloat16 [2, 4, 4, 768, 2048], P('section', 'dp', 'expert'), may hold values from -0.125 to 0.125
- w_up: bfloat16 [2, 4, 4, 768, 2048], P('section', 'dp', 'expert'), may hold values from -0.125 to 0.125
- w_down: bfloat16 [2, 4, 4, 768, 2048], P('section', 'dp', 'expert'), may hold values from -0.21875 to 0.21875
Outputs:
- input_grads: bfloat16 [2, 128, 2048], P('section', ('dp', 'expert'))
The draws below stay inside these ranges and needn't reach their ends.
Inputs may be any that keep to these rules, and one draw needn't show every extreme that they name: `routes`: within one section and stop, a token names 8 different experts, the tokens of one device name each expert at most 8 times, and some expert is named exactly 8 times by the tokens of every device.
All inputs are finite; a program needn't handle non-finite values.
Results may differ from the reference program's by a relative error of at most 0.012.
Values may be sent and summed in bfloat16 or wider, within the bound.
A program may use at most 64 MiB of HBM per device.

```python
import jax
import jax.numpy as jnp
from jax import lax

D = 2048
FF = 768
TOP = 8
STOPS = 1
TOK_DEV = 8
GROUPS = 4
SECTIONS = 2
SOURCES = 16
TOKENS = 128
EXPERTS = 16
FFP = 768
SRC_MOST = 8
N_DP = 4
N_EXPERT = 4


def draw_routes(key, part):
    rows_dev = TOK_DEV * TOP
    slot_total = SRC_MOST * EXPERTS

    def one_block(block_key):
        popular_key, hot_key, device_key = jax.random.split(block_key, 3)
        popular = jax.random.randint(popular_key, (EXPERTS,), 0, 3)
        hot_expert = jax.random.randint(hot_key, (), 0, EXPERTS)
        uplift = popular * 2048 + jnp.where(jnp.arange(EXPERTS) == hot_expert, 1 << 20, 0)

        def one_device(single_key):
            jitter_key, token_key, column_key = jax.random.split(single_key, 3)
            jitter = jax.random.randint(jitter_key, (SRC_MOST, EXPERTS), 0, 4096)
            scores = (uplift[None, :] + jitter) * slot_total + jnp.arange(slot_total).reshape(SRC_MOST, EXPERTS)
            top_scores, picked = lax.top_k(scores.reshape(-1).astype(jnp.int32), rows_dev)
            ordered = jnp.sort(picked % EXPERTS)
            sequence = ordered.reshape(TOP, TOK_DEV).T
            sequence = jax.random.permutation(token_key, sequence, axis=0)
            sequence = jax.random.permutation(column_key, sequence, axis=1, independent=True)
            return sequence.astype(jnp.int32)
        device_keys = jax.random.split(device_key, SOURCES)
        return jax.vmap(one_device)(device_keys).reshape(TOKENS, TOP)
    block_keys = jax.random.split(jax.random.fold_in(key, 17), SECTIONS * STOPS)
    return jax.vmap(one_block)(block_keys).reshape(SECTIONS, STOPS, TOKENS, TOP)


def shard_levels(key, extent, cuts, low, largest):
    gain, own = 1.0, jax.random.fold_in(key, 6)
    for dim, blocks in cuts:
        heights = jnp.exp(jax.random.uniform(jax.random.fold_in(own, dim), (blocks,), jnp.float32, low / len(cuts), largest / len(cuts)))
        gain = gain * jnp.repeat(heights, extent[dim] // blocks).reshape([-1 if axis == dim else 1 for axis in range(len(extent))])
    return gain


def centred(own_key, extent, scale, limit, pieces=(), kind=jnp.bfloat16):
    drawn = jax.random.normal(own_key, extent, jnp.float32) * scale
    if len(pieces) > 0:
        drawn = shard_levels(own_key, extent, pieces, -0.22, 0.18) * drawn
    return jnp.clip(drawn, min=-limit, max=limit).astype(kind)


def setup_inputs(seed: int = 0) -> dict:
    splits = jax.random.split(jax.random.key(seed), 8)
    cotangent = centred(splits[0], (SECTIONS, TOKENS, D), 1.0, 6.0, ((0, 2), (1, 16)))
    routes = draw_routes(jax.random.fold_in(splits[7], 71), 0)
    probs = jnp.clip(0.1 + 0.4 * jax.random.uniform(splits[2], (SECTIONS, STOPS, TOKENS, TOP), jnp.float32) ** shard_levels(splits[2], (SECTIONS, STOPS, TOKENS, TOP), ((0, 2), (2, 16)), -0.2, 0.2), 0.1, 0.5)
    stash = centred(splits[3], (SECTIONS, STOPS, N_DP, N_EXPERT, N_EXPERT, N_DP, SRC_MOST, 2 * FFP), 1.5, 6.0, ((0, 2), (2, 4), (3, 4)))
    w_gate = centred(splits[4], (SECTIONS, N_DP, N_EXPERT, FFP, D), D ** -0.5, 0.125, ((0, 2), (1, 4), (2, 4)))
    w_up = centred(splits[5], (SECTIONS, N_DP, N_EXPERT, FFP, D), D ** -0.5, 0.125, ((0, 2), (1, 4), (2, 4)))
    w_down = centred(splits[6], (SECTIONS, N_DP, N_EXPERT, FFP, D), FF ** -0.5, 0.21875, ((0, 2), (1, 4), (2, 4)))
    return dict(cotangent=cotangent, routes=routes, probs=probs, stash=stash, w_gate=w_gate, w_up=w_up, w_down=w_down)


def expert_pass(shifted, expert_ids, weights_in, saved, gate_rows, up_rows, down_rows):
    piece_count = N_EXPERT // GROUPS
    rows_dev = TOK_DEV * TOP
    flat_ids = expert_ids.reshape(SOURCES, rows_dev)
    same_id = flat_ids[:, :, None] == flat_ids[:, None, :]
    earlier = jnp.arange(rows_dev)[None, :] < jnp.arange(rows_dev)[:, None]
    ranked = jnp.sum(jnp.logical_and(same_id, earlier[None]), axis=2).astype(jnp.int32).reshape(-1)
    chosen = expert_ids.reshape(-1).astype(jnp.int32)
    source = (jnp.arange(TOKENS * TOP) // rows_dev).astype(jnp.int32)
    source_row = source // N_EXPERT
    source_column = source % N_EXPERT
    grad_rows = (weights_in[:, :, None] * shifted[:, None, :].astype(jnp.float32)).astype(jnp.bfloat16).reshape(-1, D)
    buffer = jnp.zeros((EXPERTS, N_EXPERT, N_DP, SRC_MOST, D), jnp.bfloat16)
    buffer = buffer.at[chosen, source_column, source_row, ranked].set(grad_rows)

    def one_expert(expert):
        home_row = expert % N_DP
        group = expert // N_DP
        slot_rows = buffer[expert].reshape(-1, D).astype(jnp.float32)
        start = (group * piece_count).astype(jnp.int32)
        saved_pre = lax.dynamic_slice_in_dim(saved[home_row], start, piece_count, 0)
        saved_pre = saved_pre.reshape(piece_count, -1, 2 * FFP).astype(jnp.float32)
        gate_w = lax.dynamic_slice_in_dim(gate_rows[home_row], start, piece_count, 0).astype(jnp.float32)
        up_w = lax.dynamic_slice_in_dim(up_rows[home_row], start, piece_count, 0).astype(jnp.float32)
        down_w = lax.dynamic_slice_in_dim(down_rows[home_row], start, piece_count, 0).astype(jnp.float32)
        gate_pre = saved_pre[:, :, :FFP]
        up_pre = saved_pre[:, :, FFP:]
        grad_act = jnp.einsum('sd,pfd->psf', slot_rows, down_w)
        gate_sigmoid = jax.nn.sigmoid(gate_pre)
        grad_gate = (grad_act * up_pre * gate_sigmoid * (1.0 + gate_pre * (1.0 - gate_sigmoid))).astype(jnp.bfloat16)
        grad_up = (grad_act * gate_pre * gate_sigmoid).astype(jnp.bfloat16)
        partial_value = jnp.einsum('psf,pfd->psd', grad_gate.astype(jnp.float32), gate_w)
        partial_value = partial_value + jnp.einsum('psf,pfd->psd', grad_up.astype(jnp.float32), up_w)
        partial_value = partial_value.astype(jnp.bfloat16)
        summed = jnp.sum(partial_value.astype(jnp.float32), axis=0).astype(jnp.bfloat16)
        return summed.reshape(N_EXPERT, N_DP, SRC_MOST, D)

    results = lax.map(one_expert, jnp.arange(EXPERTS, dtype=jnp.int32))
    picked = results[chosen, source_column, source_row, ranked].astype(jnp.float32)
    summed = shifted.astype(jnp.float32) + jnp.sum(picked.reshape(TOKENS, TOP, D), axis=1)
    return summed.astype(jnp.bfloat16)


def reference(cotangent, routes, probs, stash, w_gate, w_up, w_down):
    current = cotangent
    for stop_index in range(STOPS):
        current = jnp.roll(current, -1, axis=0)
        outputs = []
        for section in range(SECTIONS):
            outputs.append(expert_pass(current[section], routes[section, stop_index], probs[section, stop_index],
                                       stash[section, stop_index], w_gate[section], w_up[section], w_down[section]))
        current = jnp.stack(outputs)
    return current
```

```python
import functools

import jax
import jax.numpy as jnp
from jax import lax
from jax.experimental import pallas as pl
from jax.experimental.pallas import tpu as pltpu
from jax.sharding import PartitionSpec as P

MESH = pl.DeviceIdType.MESH


def relay_kernel(
    sections, rows, columns, chunks,
    cot, routes, probs, stash, gate_hbm, up_hbm, down_hbm, out,
    tok, wt, stash_v, gate_v, up_v, down_v, obuf, r1, s1, r2, s2, r3,
    load_sem, a_send, a_recv, y_send, y_recv, c_send, c_recv,
    wz_send, wz_recv, wy_send, wy_recv, wc_send, wc_recv,
    p1_send, p1_recv, p2_send, p2_recv, p3_send, p3_recv,
):
    sec = lax.axis_index("section")
    row = lax.axis_index("dp")
    col = lax.axis_index("expert")
    core = lax.rem(col, 2)
    ypos = col // 2
    ycount = columns // 2
    tokens, width = cot.shape
    units = down_v.shape[0]
    slots = columns * rows * tokens
    chunk = width // chunks
    mate = (sec, row, col + 1 - 2 * core)
    before = lax.rem(sec + sections - 1, sections)
    after = lax.rem(sec + 1, sections)

    def zpeer(k):
        return lax.rem(row + k, rows)

    def zfrom(k):
        return lax.rem(row + rows - k, rows)

    def ypeer(j):
        return lax.rem(col + 2 * j, columns)

    def yfrom(j):
        return lax.rem(col + columns - 2 * j, columns)

    def remote(src, dst, send, recv, device):
        return pltpu.make_async_remote_copy(
            src_ref=src, dst_ref=dst, send_sem=send, recv_sem=recv,
            device_id=device, device_id_type=MESH,
        )

    loads = [
        pltpu.make_async_copy(stash, stash_v, load_sem.at[0]),
        pltpu.make_async_copy(down_hbm, down_v, load_sem.at[1]),
        pltpu.make_async_copy(gate_hbm, gate_v, load_sem.at[2]),
        pltpu.make_async_copy(up_hbm, up_v, load_sem.at[3]),
    ]

    barrier = pltpu.get_barrier_semaphore()
    greeted = 0
    ring = [before] if sections == 2 else [before, after]
    for other in ring:
        for k in range(rows):
            pl.semaphore_signal(barrier, inc=1, device_id=(other, zpeer(k), col), device_id_type=MESH)
            greeted += 1
    for k in range(1, rows):
        pl.semaphore_signal(barrier, inc=1, device_id=(sec, zpeer(k), col), device_id_type=MESH)
        greeted += 1
    for j in range(1, ycount):
        pl.semaphore_signal(barrier, inc=1, device_id=(sec, row, ypeer(j)), device_id_type=MESH)
        greeted += 1
    pl.semaphore_signal(barrier, inc=1, device_id=mate, device_id_type=MESH)
    greeted += 1

    for load in loads:
        load.start()

    lanes = wt.shape[3]
    lane = lax.broadcasted_iota(jnp.int32, (tokens, lanes), 1)
    tile = jnp.zeros((tokens, lanes), jnp.float32)
    for k in range(routes.shape[1]):
        tile = tile + jnp.where(routes[:, k:k + 1] == lane, probs[:, k:k + 1], 0.0)
    wt[col, row] = tile

    pl.semaphore_wait(barrier, greeted)

    sends = []

    def go(copy):
        copy.start()
        sends.append(copy)

    def a_copy(k):
        return remote(cot, tok.at[col, row], a_send.at[k], a_recv.at[k], (before, zpeer(k), col))

    def a_wait(k):
        src = zfrom(k)
        remote(cot, tok.at[col, src], a_send.at[k], a_recv.at[k], mate).wait_recv()

    for k in range(rows - 1, -1, -1):
        go(a_copy(k))
    for k in range(rows - 1, 0, -1):
        go(remote(wt.at[col, row], wt.at[col, row], wz_send.at[k], wz_recv.at[k], (sec, zpeer(k), col)))

    for k in range(rows - 1, 0, -1):
        src = wt.at[col, zfrom(k)]
        remote(src, src, wz_send.at[k], wz_recv.at[k], mate).wait_recv()
    for j in range(1, ycount):
        go(remote(wt.at[col], wt.at[col], wy_send.at[j], wy_recv.at[j], (sec, row, ypeer(j))))
    go(remote(wt.at[col], wt.at[col], wc_send.at[0], wc_recv.at[0], mate))

    for k in range(rows - 1, -1, -1):
        a_wait(k)
        block = tok.at[col, zfrom(k)]
        for j in range(1, ycount):
            go(remote(block, block, y_send.at[j, k], y_recv.at[j, k], (sec, row, ypeer(j))))
        go(remote(block, block, c_send.at[0, k], c_recv.at[0, k], mate))

    for j in range(1, ycount):
        part = wt.at[yfrom(j)]
        remote(part, part, wy_send.at[j], wy_recv.at[j], mate).wait_recv()
        go(remote(part, part, wc_send.at[j], wc_recv.at[j], mate))
    for k in range(rows - 1, -1, -1):
        for j in range(1, ycount):
            block = tok.at[yfrom(j), zfrom(k)]
            remote(block, block, y_send.at[j, k], y_recv.at[j, k], mate).wait_recv()
            go(remote(block, block, c_send.at[j, k], c_recv.at[j, k], mate))
    mate_col = col + 1 - 2 * core
    for j in range(ycount):
        part = wt.at[lax.rem(mate_col + columns - 2 * j, columns)]
        remote(part, part, wc_send.at[j], wc_recv.at[j], mate).wait_recv()

    expert = col * rows + row
    weights = wt[...].reshape(slots, lanes)
    wide = lax.broadcasted_iota(jnp.int32, (slots, lanes), 1)
    weight = jnp.sum(jnp.where(wide == expert, weights, 0.0), axis=1, keepdims=True)
    named = jnp.broadcast_to((weight > 0.0).astype(jnp.float32), (slots, slots))
    at_row = lax.broadcasted_iota(jnp.int32, (slots, slots), 0)
    at_col = lax.broadcasted_iota(jnp.int32, (slots, slots), 1)
    same = (at_row // tokens) == (at_col // tokens)
    lower = jnp.where(jnp.logical_and(same, at_col < at_row), 1.0, 0.0).astype(jnp.bfloat16)
    rank = jnp.dot(lower, named.astype(jnp.bfloat16), preferred_element_type=jnp.float32)
    spot = ((at_row // tokens) * tokens).astype(jnp.float32) + rank
    pick = jnp.where(at_col.astype(jnp.float32) == spot, named, 0.0).astype(jnp.bfloat16)
    loads[0].wait()
    saved = stash_v[...].astype(jnp.float32).reshape(slots, 2 * units).astype(jnp.bfloat16)
    saved = jnp.dot(pick, saved, preferred_element_type=jnp.float32)
    gate_pre = saved[:, :units]
    up_pre = saved[:, units:]
    sg = jax.nn.sigmoid(gate_pre)
    f_gate = up_pre * sg * (1.0 + gate_pre * (1.0 - sg))
    f_up = gate_pre * sg
    loads[1].wait()

    for k in range(rows - 1, -1, -1):
        for j in range(ycount):
            block = tok.at[lax.rem(mate_col + columns - 2 * j, columns), zfrom(k)]
            remote(block, block, c_send.at[j, k], c_recv.at[j, k], mate).wait_recv()

    moved = tok[...].astype(jnp.float32).reshape(slots, width)
    grad_rows = (moved * weight).astype(jnp.bfloat16)
    grad_act = lax.dot_general(
        grad_rows, down_v[...], (((1,), (1,)), ((), ())), preferred_element_type=jnp.float32
    )
    grad_gate = (grad_act * f_gate).astype(jnp.bfloat16)
    grad_up = (grad_act * f_up).astype(jnp.bfloat16)
    loads[2].wait()
    loads[3].wait()

    def p1(t):
        return remote(obuf.at[t, 1 - core], r1.at[t], p1_send.at[t], p1_recv.at[t], mate)

    def p2(t, j):
        return remote(s1.at[t, j], r2.at[t, j], p2_send.at[t, j], p2_recv.at[t, j], (sec, row, ypeer(j)))

    def p3(t, k):
        return remote(s2.at[t, k], r3.at[t, k], p3_send.at[t, k], p3_recv.at[t, k], (sec, zpeer(k), col))

    def f32(value):
        return value.astype(jnp.float32)

    for t in range(chunks):
        span = slice(t * chunk, (t + 1) * chunk)
        part = jnp.dot(grad_gate, gate_v[:, span], preferred_element_type=jnp.float32)
        part = part + jnp.dot(grad_up, up_v[:, span], preferred_element_type=jnp.float32)
        part = part.reshape(ycount, 2, rows, tokens, chunk).astype(jnp.bfloat16)
        obuf[t, 0] = part[:, 0]
        obuf[t, 1] = part[:, 1]
        go(p1(t))
    for t in range(chunks):
        p1(t).wait_recv()
        for j in range(1, ycount):
            y = lax.rem(ypos + j, ycount)
            s1[t, j] = (f32(obuf[t, core, y]) + f32(r1[t, y])).astype(jnp.bfloat16)
            go(p2(t, j))
    for t in range(chunks):
        for j in range(1, ycount):
            p2(t, j).wait_recv()
        for k in range(rows - 1, 0, -1):
            to = zpeer(k)
            total = f32(obuf[t, core, ypos, to]) + f32(r1[t, ypos, to])
            for j in range(1, ycount):
                total = total + f32(r2[t, j, to])
            s2[t, k] = total.astype(jnp.bfloat16)
            go(p3(t, k))
    for t in range(chunks):
        span = slice(t * chunk, (t + 1) * chunk)
        total = f32(obuf[t, core, ypos, row]) + f32(r1[t, ypos, row])
        for j in range(1, ycount):
            total = total + f32(r2[t, j, row])
        for k in range(rows - 1, 0, -1):
            p3(t, k).wait_recv()
            total = total + f32(r3[t, k])
        out[:, span] = (f32(tok[col, row, :, span]) + total).astype(jnp.bfloat16)
    for copy in sends:
        copy.wait_send()


def relay(mesh, cotangent, routes, probs, stash, w_gate, w_up, w_down):
    sections, rows, columns = (mesh.shape[name] for name in ("section", "dp", "expert"))
    tokens, width = cotangent.shape[1:]
    units = w_gate.shape[3]
    ycount = columns // 2
    lanes = -(-rows * columns // 128) * 128
    chunks = max(width // 512, 1)
    chunk = width // chunks
    bf16 = jnp.bfloat16
    dma = pltpu.SemaphoreType.DMA
    vmem = pl.BlockSpec(memory_space=pltpu.VMEM)
    hbm = pl.BlockSpec(memory_space=pl.ANY)
    out = pl.pallas_call(
        functools.partial(relay_kernel, sections, rows, columns, chunks),
        out_shape=jax.ShapeDtypeStruct((tokens, width), bf16),
        in_specs=[hbm, vmem, vmem, hbm, hbm, hbm, hbm],
        out_specs=vmem,
        scratch_shapes=[
            pltpu.VMEM((columns, rows, tokens, width), bf16),
            pltpu.VMEM((columns, rows, tokens, lanes), jnp.float32),
            pltpu.VMEM((columns, rows, tokens, 2 * units), bf16),
            pltpu.VMEM((units, width), bf16),
            pltpu.VMEM((units, width), bf16),
            pltpu.VMEM((units, width), bf16),
            pltpu.VMEM((chunks, 2, ycount, rows, tokens, chunk), bf16),
            pltpu.VMEM((chunks, ycount, rows, tokens, chunk), bf16),
            pltpu.VMEM((chunks, ycount, rows, tokens, chunk), bf16),
            pltpu.VMEM((chunks, ycount, rows, tokens, chunk), bf16),
            pltpu.VMEM((chunks, rows, tokens, chunk), bf16),
            pltpu.VMEM((chunks, rows, tokens, chunk), bf16),
            dma((4,)),
            dma((rows,)), dma((rows,)),
            dma((ycount, rows)), dma((ycount, rows)),
            dma((ycount, rows)), dma((ycount, rows)),
            dma((rows,)), dma((rows,)),
            dma((ycount,)), dma((ycount,)),
            dma((ycount,)), dma((ycount,)),
            dma((chunks,)), dma((chunks,)),
            dma((chunks, ycount)), dma((chunks, ycount)),
            dma((chunks, rows)), dma((chunks, rows)),
        ],
        compiler_params=pltpu.CompilerParams(collective_id=0, has_side_effects=True),
    )(
        cotangent[0], routes[0, 0], probs[0, 0],
        stash.reshape(columns, rows, tokens, 2 * units),
        w_gate[0, 0, 0], w_up[0, 0, 0], w_down[0, 0, 0],
    )
    return out[None]


def shifted_2(value, axis, steps):
    count = lax.axis_size(axis)
    pairs = [(source, (source + steps) % count) for source in range(count)]
    return lax.ppermute(value, axis, pairs)


def body(mesh, cotangent, routes, probs, stash, w_gate, w_up, w_down):
    if (
        mesh.shape["expert"] in (2, 4)
        and stash.shape[6] == cotangent.shape[1]
    ):
        return relay(mesh, cotangent, routes, probs, stash, w_gate, w_up, w_down)
    row_count = lax.axis_size("dp")
    column_count = lax.axis_size("expert")
    group_count = min(4, column_count)
    piece_count = column_count // group_count
    expert_count = group_count * row_count
    slot_most = stash.shape[6]
    model_width = w_gate.shape[4]
    piece_units = w_gate.shape[3]
    token_count = cotangent.shape[1]
    top_count = routes.shape[3]
    rows_dev = token_count * top_count
    code_count = expert_count * slot_most
    gate_piece = w_gate[0, 0, 0]
    up_piece = w_up[0, 0, 0]
    down_piece = w_down[0, 0, 0]
    earlier = lax.broadcasted_iota(jnp.int32, (rows_dev, rows_dev), 1) < lax.broadcasted_iota(
        jnp.int32, (rows_dev, rows_dev), 0
    )
    code_grid = lax.broadcasted_iota(jnp.int32, (rows_dev, code_count), 1)
    current = cotangent[0]
    shifted = shifted_2(current, "section", -1)
    expert_ids = routes[0, 0].reshape(-1)
    same_id = expert_ids[:, None] == expert_ids[None, :]
    ranked = jnp.sum(jnp.logical_and(same_id, earlier), axis=1)
    slot_code = expert_ids * slot_most + ranked
    selector = (slot_code[:, None] == code_grid).astype(jnp.bfloat16)
    grad_rows = (probs[0, 0][:, :, None] * shifted[:, None, :].astype(jnp.float32)).astype(
        jnp.bfloat16
    )
    grad_rows = grad_rows.reshape(rows_dev, model_width)
    packed = lax.dot_general(
        selector, grad_rows, (((0,), (0,)), ((), ())), preferred_element_type=jnp.float32
    )
    outgoing = packed.astype(jnp.bfloat16).reshape(group_count, row_count, slot_most, model_width)
    arrived = lax.all_to_all(outgoing, "dp", split_axis=1, concat_axis=1, tiled=True)
    copies = jnp.broadcast_to(
        arrived[:, None], (group_count, piece_count, row_count, slot_most, model_width)
    )
    copies = copies.reshape(column_count, row_count, slot_most, model_width)
    owned = lax.all_to_all(copies, "expert", split_axis=0, concat_axis=0, tiled=True)
    slot_rows = owned.reshape(-1, model_width)
    saved_pre = stash[0, 0, 0, 0].reshape(-1, 2 * piece_units)
    gate_pre = saved_pre[:, :piece_units].astype(jnp.float32)
    up_pre = saved_pre[:, piece_units:].astype(jnp.float32)
    grad_act = lax.dot_general(
        slot_rows, down_piece, (((1,), (1,)), ((), ())), preferred_element_type=jnp.float32
    )
    gate_sigmoid = jax.nn.sigmoid(gate_pre)
    grad_gate = (grad_act * up_pre * gate_sigmoid * (1.0 + gate_pre * (1.0 - gate_sigmoid))).astype(
        jnp.bfloat16
    )
    grad_up = (grad_act * gate_pre * gate_sigmoid).astype(jnp.bfloat16)
    partial_value = jnp.dot(grad_gate, gate_piece, preferred_element_type=jnp.float32)
    partial_value = (
        partial_value + jnp.dot(grad_up, up_piece, preferred_element_type=jnp.float32)
    ).astype(jnp.bfloat16)
    returned = lax.all_to_all(
        partial_value.reshape(column_count, row_count, slot_most, model_width),
        "expert",
        split_axis=0,
        concat_axis=0,
        tiled=True,
    )
    returned = returned.reshape(group_count, piece_count, row_count, slot_most, model_width)
    summed = jnp.sum(returned, axis=1, dtype=jnp.float32).astype(jnp.bfloat16)
    returned_rows = lax.all_to_all(summed, "dp", split_axis=1, concat_axis=1, tiled=True)
    token_select = jnp.sum(selector.reshape(token_count, top_count, code_count), axis=1)
    gathered = jnp.dot(
        token_select,
        returned_rows.reshape(code_count, model_width),
        preferred_element_type=jnp.float32,
    )
    current = (shifted.astype(jnp.float32) + gathered).astype(jnp.bfloat16)
    return current[None]


def solution(mesh):
    placed = (
        P("section", ("dp", "expert"), None),
        P("section", None, ("dp", "expert"), None),
        P("section", None, ("dp", "expert"), None),
        P("section", None, "dp", "expert", None, None, None, None),
        P("section", "dp", "expert", None, None),
        P("section", "dp", "expert", None, None),
        P("section", "dp", "expert", None, None),
    )
    return jax.shard_map(
        functools.partial(body, mesh),
        mesh=mesh,
        in_specs=placed,
        out_specs=P("section", ("dp", "expert"), None),
        check_vma=False,
    )
```

```python
import functools

import jax
import jax.numpy as jnp
from jax import lax
from jax.experimental import pallas as pl
from jax.experimental.pallas import tpu as pltpu
from jax.sharding import PartitionSpec as P

MESH = pl.DeviceIdType.MESH


def relay_kernel(
    sections, rows, columns, chunks,
    cot, routes_hbm, probs_hbm, stash, gate_hbm, up_hbm, down_hbm, out,
    routes, probs, tok, wt, stash_v, gate_v, up_v, down_v, obuf, r1, s1, r2, s2, r3,
    load_sem, a_send, a_recv, y_send, y_recv, c_send, c_recv,
    wz_send, wz_recv, wy_send, wy_recv, wc_send, wc_recv,
    p1_send, p1_recv, p2_send, p2_recv, p3_send, p3_recv,
):
    sec = lax.axis_index("section")
    row = lax.axis_index("dp")
    col = lax.axis_index("expert")
    core = lax.rem(col, 2)
    ypos = col // 2
    ycount = columns // 2
    tokens, width = cot.shape
    units = down_v.shape[0]
    slots = columns * rows * tokens
    chunk = width // chunks
    mate = (sec, row, col + 1 - 2 * core)
    before = lax.rem(sec + sections - 1, sections)
    after = lax.rem(sec + 1, sections)

    def zpeer(k):
        return lax.rem(row + k, rows)

    def zfrom(k):
        return lax.rem(row + rows - k, rows)

    def ypeer(j):
        return lax.rem(col + 2 * j, columns)

    def yfrom(j):
        return lax.rem(col + columns - 2 * j, columns)

    def remote(src, dst, send, recv, device):
        return pltpu.make_async_remote_copy(
            src_ref=src, dst_ref=dst, send_sem=send, recv_sem=recv,
            device_id=device, device_id_type=MESH,
        )

    small = [
        pltpu.make_async_copy(routes_hbm, routes, load_sem.at[4]),
        pltpu.make_async_copy(probs_hbm, probs, load_sem.at[5]),
    ]
    loads = [
        pltpu.make_async_copy(stash, stash_v, load_sem.at[0]),
        pltpu.make_async_copy(down_hbm, down_v, load_sem.at[1]),
        pltpu.make_async_copy(gate_hbm, gate_v, load_sem.at[2]),
        pltpu.make_async_copy(up_hbm, up_v, load_sem.at[3]),
    ]

    for load in small:
        load.start()
    barrier = pltpu.get_barrier_semaphore()
    greeted = 0
    ring = [before] if sections == 2 else [before, after]
    for other in ring:
        for k in range(rows):
            pl.semaphore_signal(barrier, inc=1, device_id=(other, zpeer(k), col), device_id_type=MESH)
            greeted += 1
    for k in range(1, rows):
        pl.semaphore_signal(barrier, inc=1, device_id=(sec, zpeer(k), col), device_id_type=MESH)
        greeted += 1
    for j in range(1, ycount):
        pl.semaphore_signal(barrier, inc=1, device_id=(sec, row, ypeer(j)), device_id_type=MESH)
        greeted += 1
    pl.semaphore_signal(barrier, inc=1, device_id=mate, device_id_type=MESH)
    greeted += 1

    for load in loads:
        load.start()

    for load in small:
        load.wait()
    lanes = wt.shape[3]
    lane = lax.broadcasted_iota(jnp.int32, (tokens, lanes), 1)
    tile = jnp.zeros((tokens, lanes), jnp.float32)
    for k in range(routes.shape[1]):
        tile = tile + jnp.where(routes[:, k:k + 1] == lane, probs[:, k:k + 1], 0.0)
    wt[col, row] = tile

    pl.semaphore_wait(barrier, greeted)

    sends = []

    def go(copy):
        copy.start()
        sends.append(copy)

    def a_copy(k):
        return remote(cot, tok.at[col, row], a_send.at[k], a_recv.at[k], (before, zpeer(k), col))

    def a_wait(k):
        src = zfrom(k)
        remote(cot, tok.at[col, src], a_send.at[k], a_recv.at[k], mate).wait_recv()

    for k in range(rows - 1, -1, -1):
        go(a_copy(k))
    for k in range(rows - 1, 0, -1):
        go(remote(wt.at[col, row], wt.at[col, row], wz_send.at[k], wz_recv.at[k], (sec, zpeer(k), col)))

    for k in range(rows - 1, 0, -1):
        src = wt.at[col, zfrom(k)]
        remote(src, src, wz_send.at[k], wz_recv.at[k], mate).wait_recv()
    for j in range(1, ycount):
        go(remote(wt.at[col], wt.at[col], wy_send.at[j], wy_recv.at[j], (sec, row, ypeer(j))))
    go(remote(wt.at[col], wt.at[col], wc_send.at[0], wc_recv.at[0], mate))

    for k in range(rows - 1, -1, -1):
        a_wait(k)
        block = tok.at[col, zfrom(k)]
        for j in range(1, ycount):
            go(remote(block, block, y_send.at[j, k], y_recv.at[j, k], (sec, row, ypeer(j))))
        go(remote(block, block, c_send.at[0, k], c_recv.at[0, k], mate))

    for j in range(1, ycount):
        part = wt.at[yfrom(j)]
        remote(part, part, wy_send.at[j], wy_recv.at[j], mate).wait_recv()
        go(remote(part, part, wc_send.at[j], wc_recv.at[j], mate))
    for k in range(rows - 1, -1, -1):
        for j in range(1, ycount):
            block = tok.at[yfrom(j), zfrom(k)]
            remote(block, block, y_send.at[j, k], y_recv.at[j, k], mate).wait_recv()
            go(remote(block, block, c_send.at[j, k], c_recv.at[j, k], mate))
    mate_col = col + 1 - 2 * core
    for j in range(ycount):
        part = wt.at[lax.rem(mate_col + columns - 2 * j, columns)]
        remote(part, part, wc_send.at[j], wc_recv.at[j], mate).wait_recv()

    expert = col * rows + row
    weights = wt[...].reshape(slots, lanes)
    wide = lax.broadcasted_iota(jnp.int32, (slots, lanes), 1)
    weight = jnp.sum(jnp.where(wide == expert, weights, 0.0), axis=1, keepdims=True)
    named = jnp.broadcast_to((weight > 0.0).astype(jnp.float32), (slots, slots))
    at_row = lax.broadcasted_iota(jnp.int32, (slots, slots), 0)
    at_col = lax.broadcasted_iota(jnp.int32, (slots, slots), 1)
    same = (at_row // tokens) == (at_col // tokens)
    lower = jnp.where(jnp.logical_and(same, at_col < at_row), 1.0, 0.0).astype(jnp.bfloat16)
    rank = jnp.dot(lower, named.astype(jnp.bfloat16), preferred_element_type=jnp.float32)
    spot = ((at_row // tokens) * tokens).astype(jnp.float32) + rank
    pick = jnp.where(at_col.astype(jnp.float32) == spot, named, 0.0).astype(jnp.bfloat16)
    loads[0].wait()
    saved = stash_v[...].astype(jnp.float32).reshape(slots, 2 * units).astype(jnp.bfloat16)
    saved = jnp.dot(pick, saved, preferred_element_type=jnp.float32)
    gate_pre = saved[:, :units]
    up_pre = saved[:, units:]
    sg = jax.nn.sigmoid(gate_pre)
    f_gate = up_pre * sg * (1.0 + gate_pre * (1.0 - sg))
    f_up = gate_pre * sg
    loads[1].wait()

    for k in range(rows - 1, -1, -1):
        for j in range(ycount):
            block = tok.at[lax.rem(mate_col + columns - 2 * j, columns), zfrom(k)]
            remote(block, block, c_send.at[j, k], c_recv.at[j, k], mate).wait_recv()

    moved = tok[...].astype(jnp.float32).reshape(slots, width)
    grad_rows = (moved * weight).astype(jnp.bfloat16)
    grad_act = lax.dot_general(
        grad_rows, down_v[...], (((1,), (1,)), ((), ())), preferred_element_type=jnp.float32
    )
    grad_gate = (grad_act * f_gate).astype(jnp.bfloat16)
    grad_up = (grad_act * f_up).astype(jnp.bfloat16)
    loads[2].wait()
    loads[3].wait()

    def p1(t):
        return remote(obuf.at[t, 1 - core], r1.at[t], p1_send.at[t], p1_recv.at[t], mate)

    def p2(t, j):
        return remote(s1.at[t, j], r2.at[t, j], p2_send.at[t, j], p2_recv.at[t, j], (sec, row, ypeer(j)))

    def p3(t, k):
        return remote(s2.at[t, k], r3.at[t, k], p3_send.at[t, k], p3_recv.at[t, k], (sec, zpeer(k), col))

    def f32(value):
        return value.astype(jnp.float32)

    for t in range(chunks):
        span = slice(t * chunk, (t + 1) * chunk)
        part = jnp.dot(grad_gate, gate_v[:, span], preferred_element_type=jnp.float32)
        part = part + jnp.dot(grad_up, up_v[:, span], preferred_element_type=jnp.float32)
        part = part.reshape(ycount, 2, rows, tokens, chunk).astype(jnp.bfloat16)
        obuf[t, 0] = part[:, 0]
        obuf[t, 1] = part[:, 1]
        go(p1(t))
    for t in range(chunks):
        p1(t).wait_recv()
        for j in range(1, ycount):
            y = lax.rem(ypos + j, ycount)
            s1[t, j] = (f32(obuf[t, core, y]) + f32(r1[t, y])).astype(jnp.bfloat16)
            go(p2(t, j))
    for t in range(chunks):
        for j in range(1, ycount):
            p2(t, j).wait_recv()
        for k in range(rows - 1, 0, -1):
            to = zpeer(k)
            total = f32(obuf[t, core, ypos, to]) + f32(r1[t, ypos, to])
            for j in range(1, ycount):
                total = total + f32(r2[t, j, to])
            s2[t, k] = total.astype(jnp.bfloat16)
            go(p3(t, k))
    for t in range(chunks):
        span = slice(t * chunk, (t + 1) * chunk)
        total = f32(obuf[t, core, ypos, row]) + f32(r1[t, ypos, row])
        for j in range(1, ycount):
            total = total + f32(r2[t, j, row])
        for k in range(rows - 1, 0, -1):
            p3(t, k).wait_recv()
            total = total + f32(r3[t, k])
        out[:, span] = (f32(tok[col, row, :, span]) + total).astype(jnp.bfloat16)
    for copy in sends:
        copy.wait_send()


def relay(mesh, cotangent, routes, probs, stash, w_gate, w_up, w_down):
    sections, rows, columns = (mesh.shape[name] for name in ("section", "dp", "expert"))
    tokens, width = cotangent.shape[1:]
    units = w_gate.shape[3]
    ycount = columns // 2
    lanes = -(-rows * columns // 128) * 128
    chunks = max(width // 512, 1)
    chunk = width // chunks
    bf16 = jnp.bfloat16
    dma = pltpu.SemaphoreType.DMA
    vmem = pl.BlockSpec(memory_space=pltpu.VMEM)
    hbm = pl.BlockSpec(memory_space=pl.ANY)
    out = pl.pallas_call(
        functools.partial(relay_kernel, sections, rows, columns, chunks),
        out_shape=pltpu.VMEM((tokens, width), bf16),
        in_specs=[hbm, hbm, hbm, hbm, hbm, hbm, hbm],
        out_specs=vmem,
        scratch_shapes=[
            pltpu.VMEM(routes.shape[2:], jnp.int32),
            pltpu.VMEM(probs.shape[2:], jnp.float32),
            pltpu.VMEM((columns, rows, tokens, width), bf16),
            pltpu.VMEM((columns, rows, tokens, lanes), jnp.float32),
            pltpu.VMEM((columns, rows, tokens, 2 * units), bf16),
            pltpu.VMEM((units, width), bf16),
            pltpu.VMEM((units, width), bf16),
            pltpu.VMEM((units, width), bf16),
            pltpu.VMEM((chunks, 2, ycount, rows, tokens, chunk), bf16),
            pltpu.VMEM((chunks, ycount, rows, tokens, chunk), bf16),
            pltpu.VMEM((chunks, ycount, rows, tokens, chunk), bf16),
            pltpu.VMEM((chunks, ycount, rows, tokens, chunk), bf16),
            pltpu.VMEM((chunks, rows, tokens, chunk), bf16),
            pltpu.VMEM((chunks, rows, tokens, chunk), bf16),
            dma((6,)),
            dma((rows,)), dma((rows,)),
            dma((ycount, rows)), dma((ycount, rows)),
            dma((ycount, rows)), dma((ycount, rows)),
            dma((rows,)), dma((rows,)),
            dma((ycount,)), dma((ycount,)),
            dma((ycount,)), dma((ycount,)),
            dma((chunks,)), dma((chunks,)),
            dma((chunks, ycount)), dma((chunks, ycount)),
            dma((chunks, rows)), dma((chunks, rows)),
        ],
        compiler_params=pltpu.CompilerParams(collective_id=0, has_side_effects=True),
    )(
        cotangent[0], routes[0, 0], probs[0, 0],
        stash.reshape(columns, rows, tokens, 2 * units),
        w_gate[0, 0, 0], w_up[0, 0, 0], w_down[0, 0, 0],
    )
    return out[None]


def shifted_2(value, axis, steps):
    count = lax.axis_size(axis)
    pairs = [(source, (source + steps) % count) for source in range(count)]
    return lax.ppermute(value, axis, pairs)


def body(mesh, cotangent, routes, probs, stash, w_gate, w_up, w_down):
    if (
        mesh.shape["expert"] in (2, 4)
        and stash.shape[6] == cotangent.shape[1]
    ):
        return relay(mesh, cotangent, routes, probs, stash, w_gate, w_up, w_down)
    row_count = lax.axis_size("dp")
    column_count = lax.axis_size("expert")
    group_count = min(4, column_count)
    piece_count = column_count // group_count
    expert_count = group_count * row_count
    slot_most = stash.shape[6]
    model_width = w_gate.shape[4]
    piece_units = w_gate.shape[3]
    token_count = cotangent.shape[1]
    top_count = routes.shape[3]
    rows_dev = token_count * top_count
    code_count = expert_count * slot_most
    gate_piece = w_gate[0, 0, 0]
    up_piece = w_up[0, 0, 0]
    down_piece = w_down[0, 0, 0]
    earlier = lax.broadcasted_iota(jnp.int32, (rows_dev, rows_dev), 1) < lax.broadcasted_iota(
        jnp.int32, (rows_dev, rows_dev), 0
    )
    code_grid = lax.broadcasted_iota(jnp.int32, (rows_dev, code_count), 1)
    current = cotangent[0]
    shifted = shifted_2(current, "section", -1)
    expert_ids = routes[0, 0].reshape(-1)
    same_id = expert_ids[:, None] == expert_ids[None, :]
    ranked = jnp.sum(jnp.logical_and(same_id, earlier), axis=1)
    slot_code = expert_ids * slot_most + ranked
    selector = (slot_code[:, None] == code_grid).astype(jnp.bfloat16)
    grad_rows = (probs[0, 0][:, :, None] * shifted[:, None, :].astype(jnp.float32)).astype(
        jnp.bfloat16
    )
    grad_rows = grad_rows.reshape(rows_dev, model_width)
    packed = lax.dot_general(
        selector, grad_rows, (((0,), (0,)), ((), ())), preferred_element_type=jnp.float32
    )
    outgoing = packed.astype(jnp.bfloat16).reshape(group_count, row_count, slot_most, model_width)
    arrived = lax.all_to_all(outgoing, "dp", split_axis=1, concat_axis=1, tiled=True)
    copies = jnp.broadcast_to(
        arrived[:, None], (group_count, piece_count, row_count, slot_most, model_width)
    )
    copies = copies.reshape(column_count, row_count, slot_most, model_width)
    owned = lax.all_to_all(copies, "expert", split_axis=0, concat_axis=0, tiled=True)
    slot_rows = owned.reshape(-1, model_width)
    saved_pre = stash[0, 0, 0, 0].reshape(-1, 2 * piece_units)
    gate_pre = saved_pre[:, :piece_units].astype(jnp.float32)
    up_pre = saved_pre[:, piece_units:].astype(jnp.float32)
    grad_act = lax.dot_general(
        slot_rows, down_piece, (((1,), (1,)), ((), ())), preferred_element_type=jnp.float32
    )
    gate_sigmoid = jax.nn.sigmoid(gate_pre)
    grad_gate = (grad_act * up_pre * gate_sigmoid * (1.0 + gate_pre * (1.0 - gate_sigmoid))).astype(
        jnp.bfloat16
    )
    grad_up = (grad_act * gate_pre * gate_sigmoid).astype(jnp.bfloat16)
    partial_value = jnp.dot(grad_gate, gate_piece, preferred_element_type=jnp.float32)
    partial_value = (
        partial_value + jnp.dot(grad_up, up_piece, preferred_element_type=jnp.float32)
    ).astype(jnp.bfloat16)
    returned = lax.all_to_all(
        partial_value.reshape(column_count, row_count, slot_most, model_width),
        "expert",
        split_axis=0,
        concat_axis=0,
        tiled=True,
    )
    returned = returned.reshape(group_count, piece_count, row_count, slot_most, model_width)
    summed = jnp.sum(returned, axis=1, dtype=jnp.float32).astype(jnp.bfloat16)
    returned_rows = lax.all_to_all(summed, "dp", split_axis=1, concat_axis=1, tiled=True)
    token_select = jnp.sum(selector.reshape(token_count, top_count, code_count), axis=1)
    gathered = jnp.dot(
        token_select,
        returned_rows.reshape(code_count, model_width),
        preferred_element_type=jnp.float32,
    )
    current = (shifted.astype(jnp.float32) + gathered).astype(jnp.bfloat16)
    return current[None]


def solution(mesh):
    placed = (
        P("section", ("dp", "expert"), None),
        P("section", None, ("dp", "expert"), None),
        P("section", None, ("dp", "expert"), None),
        P("section", None, "dp", "expert", None, None, None, None),
        P("section", "dp", "expert", None, None),
        P("section", "dp", "expert", None, None),
        P("section", "dp", "expert", None, None),
    )
    return jax.shard_map(
        functools.partial(body, mesh),
        mesh=mesh,
        in_specs=placed,
        out_specs=P("section", ("dp", "expert"), None),
        check_vma=False,
    )
```

```python
import functools

import jax
import jax.numpy as jnp
from jax import lax
from jax.experimental import pallas as pl
from jax.experimental.pallas import tpu as pltpu
from jax.sharding import PartitionSpec as P

MESH = pl.DeviceIdType.MESH


def relay_kernel(
    sections, rows, columns, chunks,
    cot_hbm, routes_hbm, probs_hbm, stash, gate_hbm, up_hbm, down_hbm, out,
    cot, routes, probs, tok, wt, stash_v, gate_v, up_v, down_v, obuf, r1, s1, r2, s2, r3,
    load_sem, a_send, a_recv, y_send, y_recv, c_send, c_recv,
    wz_send, wz_recv, wy_send, wy_recv, wc_send, wc_recv,
    p1_send, p1_recv, p2_send, p2_recv, p3_send, p3_recv,
):
    sec = lax.axis_index("section")
    row = lax.axis_index("dp")
    col = lax.axis_index("expert")
    core = lax.rem(col, 2)
    ypos = col // 2
    ycount = columns // 2
    tokens, width = cot.shape
    units = down_v.shape[0]
    slots = columns * rows * tokens
    chunk = width // chunks
    mate = (sec, row, col + 1 - 2 * core)
    before = lax.rem(sec + sections - 1, sections)
    after = lax.rem(sec + 1, sections)

    def zpeer(k):
        return lax.rem(row + k, rows)

    def zfrom(k):
        return lax.rem(row + rows - k, rows)

    def ypeer(j):
        return lax.rem(col + 2 * j, columns)

    def yfrom(j):
        return lax.rem(col + columns - 2 * j, columns)

    def remote(src, dst, send, recv, device):
        return pltpu.make_async_remote_copy(
            src_ref=src, dst_ref=dst, send_sem=send, recv_sem=recv,
            device_id=device, device_id_type=MESH,
        )

    small = [
        pltpu.make_async_copy(cot_hbm, cot, load_sem.at[6]),
        pltpu.make_async_copy(routes_hbm, routes, load_sem.at[4]),
        pltpu.make_async_copy(probs_hbm, probs, load_sem.at[5]),
    ]
    loads = [
        pltpu.make_async_copy(stash, stash_v, load_sem.at[0]),
        pltpu.make_async_copy(down_hbm, down_v, load_sem.at[1]),
        pltpu.make_async_copy(gate_hbm, gate_v, load_sem.at[2]),
        pltpu.make_async_copy(up_hbm, up_v, load_sem.at[3]),
    ]

    for load in small:
        load.start()
    barrier = pltpu.get_barrier_semaphore()
    greeted = 0
    ring = [before] if sections == 2 else [before, after]
    for other in ring:
        for k in range(rows):
            pl.semaphore_signal(barrier, inc=1, device_id=(other, zpeer(k), col), device_id_type=MESH)
            greeted += 1
    for k in range(1, rows):
        pl.semaphore_signal(barrier, inc=1, device_id=(sec, zpeer(k), col), device_id_type=MESH)
        greeted += 1
    for j in range(1, ycount):
        pl.semaphore_signal(barrier, inc=1, device_id=(sec, row, ypeer(j)), device_id_type=MESH)
        greeted += 1
    pl.semaphore_signal(barrier, inc=1, device_id=mate, device_id_type=MESH)
    greeted += 1

    for load in loads:
        load.start()

    for load in small:
        load.wait()
    lanes = wt.shape[3]
    lane = lax.broadcasted_iota(jnp.int32, (tokens, lanes), 1)
    tile = jnp.zeros((tokens, lanes), jnp.float32)
    for k in range(routes.shape[1]):
        tile = tile + jnp.where(routes[:, k:k + 1] == lane, probs[:, k:k + 1], 0.0)
    wt[col, row] = tile

    pl.semaphore_wait(barrier, greeted)

    sends = []

    def go(copy):
        copy.start()
        sends.append(copy)

    def a_copy(k):
        return remote(cot, tok.at[col, row], a_send.at[k], a_recv.at[k], (before, zpeer(k), col))

    def a_wait(k):
        src = zfrom(k)
        remote(cot, tok.at[col, src], a_send.at[k], a_recv.at[k], mate).wait_recv()

    for k in range(rows - 1, -1, -1):
        go(a_copy(k))
    for k in range(rows - 1, 0, -1):
        go(remote(wt.at[col, row], wt.at[col, row], wz_send.at[k], wz_recv.at[k], (sec, zpeer(k), col)))

    for k in range(rows - 1, 0, -1):
        src = wt.at[col, zfrom(k)]
        remote(src, src, wz_send.at[k], wz_recv.at[k], mate).wait_recv()
    for j in range(1, ycount):
        go(remote(wt.at[col], wt.at[col], wy_send.at[j], wy_recv.at[j], (sec, row, ypeer(j))))
    go(remote(wt.at[col], wt.at[col], wc_send.at[0], wc_recv.at[0], mate))

    for k in range(rows - 1, -1, -1):
        a_wait(k)
        block = tok.at[col, zfrom(k)]
        for j in range(1, ycount):
            go(remote(block, block, y_send.at[j, k], y_recv.at[j, k], (sec, row, ypeer(j))))
        go(remote(block, block, c_send.at[0, k], c_recv.at[0, k], mate))

    for j in range(1, ycount):
        part = wt.at[yfrom(j)]
        remote(part, part, wy_send.at[j], wy_recv.at[j], mate).wait_recv()
        go(remote(part, part, wc_send.at[j], wc_recv.at[j], mate))
    for k in range(rows - 1, -1, -1):
        for j in range(1, ycount):
            block = tok.at[yfrom(j), zfrom(k)]
            remote(block, block, y_send.at[j, k], y_recv.at[j, k], mate).wait_recv()
            go(remote(block, block, c_send.at[j, k], c_recv.at[j, k], mate))
    mate_col = col + 1 - 2 * core
    for j in range(ycount):
        part = wt.at[lax.rem(mate_col + columns - 2 * j, columns)]
        remote(part, part, wc_send.at[j], wc_recv.at[j], mate).wait_recv()

    expert = col * rows + row
    weights = wt[...].reshape(slots, lanes)
    wide = lax.broadcasted_iota(jnp.int32, (slots, lanes), 1)
    weight = jnp.sum(jnp.where(wide == expert, weights, 0.0), axis=1, keepdims=True)
    named = jnp.broadcast_to((weight > 0.0).astype(jnp.float32), (slots, slots))
    at_row = lax.broadcasted_iota(jnp.int32, (slots, slots), 0)
    at_col = lax.broadcasted_iota(jnp.int32, (slots, slots), 1)
    same = (at_row // tokens) == (at_col // tokens)
    lower = jnp.where(jnp.logical_and(same, at_col < at_row), 1.0, 0.0).astype(jnp.bfloat16)
    rank = jnp.dot(lower, named.astype(jnp.bfloat16), preferred_element_type=jnp.float32)
    spot = ((at_row // tokens) * tokens).astype(jnp.float32) + rank
    pick = jnp.where(at_col.astype(jnp.float32) == spot, named, 0.0).astype(jnp.bfloat16)
    loads[0].wait()
    saved = stash_v[...].astype(jnp.float32).reshape(slots, 2 * units).astype(jnp.bfloat16)
    saved = jnp.dot(pick, saved, preferred_element_type=jnp.float32)
    gate_pre = saved[:, :units]
    up_pre = saved[:, units:]
    sg = jax.nn.sigmoid(gate_pre)
    f_gate = up_pre * sg * (1.0 + gate_pre * (1.0 - sg))
    f_up = gate_pre * sg
    loads[1].wait()

    for k in range(rows - 1, -1, -1):
        for j in range(ycount):
            block = tok.at[lax.rem(mate_col + columns - 2 * j, columns), zfrom(k)]
            remote(block, block, c_send.at[j, k], c_recv.at[j, k], mate).wait_recv()

    moved = tok[...].astype(jnp.float32).reshape(slots, width)
    grad_rows = (moved * weight).astype(jnp.bfloat16)
    grad_act = lax.dot_general(
        grad_rows, down_v[...], (((1,), (1,)), ((), ())), preferred_element_type=jnp.float32
    )
    grad_gate = (grad_act * f_gate).astype(jnp.bfloat16)
    grad_up = (grad_act * f_up).astype(jnp.bfloat16)
    loads[2].wait()
    loads[3].wait()

    def p1(t):
        return remote(obuf.at[t, 1 - core], r1.at[t], p1_send.at[t], p1_recv.at[t], mate)

    def p2(t, j):
        return remote(s1.at[t, j], r2.at[t, j], p2_send.at[t, j], p2_recv.at[t, j], (sec, row, ypeer(j)))

    def p3(t, k):
        return remote(s2.at[t, k], r3.at[t, k], p3_send.at[t, k], p3_recv.at[t, k], (sec, zpeer(k), col))

    def f32(value):
        return value.astype(jnp.float32)

    for t in range(chunks):
        span = slice(t * chunk, (t + 1) * chunk)
        part = jnp.dot(grad_gate, gate_v[:, span], preferred_element_type=jnp.float32)
        part = part + jnp.dot(grad_up, up_v[:, span], preferred_element_type=jnp.float32)
        part = part.reshape(ycount, 2, rows, tokens, chunk).astype(jnp.bfloat16)
        obuf[t, 0] = part[:, 0]
        obuf[t, 1] = part[:, 1]
        go(p1(t))
    for t in range(chunks):
        p1(t).wait_recv()
        for j in range(1, ycount):
            y = lax.rem(ypos + j, ycount)
            s1[t, j] = (f32(obuf[t, core, y]) + f32(r1[t, y])).astype(jnp.bfloat16)
            go(p2(t, j))
    for t in range(chunks):
        for j in range(1, ycount):
            p2(t, j).wait_recv()
        for k in range(rows - 1, 0, -1):
            to = zpeer(k)
            total = f32(obuf[t, core, ypos, to]) + f32(r1[t, ypos, to])
            for j in range(1, ycount):
                total = total + f32(r2[t, j, to])
            s2[t, k] = total.astype(jnp.bfloat16)
            go(p3(t, k))
    for t in range(chunks):
        span = slice(t * chunk, (t + 1) * chunk)
        total = f32(obuf[t, core, ypos, row]) + f32(r1[t, ypos, row])
        for j in range(1, ycount):
            total = total + f32(r2[t, j, row])
        for k in range(rows - 1, 0, -1):
            p3(t, k).wait_recv()
            total = total + f32(r3[t, k])
        out[:, span] = (f32(tok[col, row, :, span]) + total).astype(jnp.bfloat16)
    for copy in sends:
        copy.wait_send()


def relay(mesh, cotangent, routes, probs, stash, w_gate, w_up, w_down):
    sections, rows, columns = (mesh.shape[name] for name in ("section", "dp", "expert"))
    tokens, width = cotangent.shape[1:]
    units = w_gate.shape[3]
    ycount = columns // 2
    lanes = -(-rows * columns // 128) * 128
    chunks = max(width // 1024, 1)
    chunk = width // chunks
    bf16 = jnp.bfloat16
    dma = pltpu.SemaphoreType.DMA
    vmem = pl.BlockSpec(memory_space=pltpu.VMEM)
    hbm = pl.BlockSpec(memory_space=pl.ANY)
    out = pl.pallas_call(
        functools.partial(relay_kernel, sections, rows, columns, chunks),
        out_shape=pltpu.VMEM((tokens, width), bf16),
        in_specs=[hbm, hbm, hbm, hbm, hbm, hbm, hbm],
        out_specs=vmem,
        scratch_shapes=[
            pltpu.VMEM((tokens, width), bf16),
            pltpu.VMEM(routes.shape[2:], jnp.int32),
            pltpu.VMEM(probs.shape[2:], jnp.float32),
            pltpu.VMEM((columns, rows, tokens, width), bf16),
            pltpu.VMEM((columns, rows, tokens, lanes), jnp.float32),
            pltpu.VMEM((columns, rows, tokens, 2 * units), bf16),
            pltpu.VMEM((units, width), bf16),
            pltpu.VMEM((units, width), bf16),
            pltpu.VMEM((units, width), bf16),
            pltpu.VMEM((chunks, 2, ycount, rows, tokens, chunk), bf16),
            pltpu.VMEM((chunks, ycount, rows, tokens, chunk), bf16),
            pltpu.VMEM((chunks, ycount, rows, tokens, chunk), bf16),
            pltpu.VMEM((chunks, ycount, rows, tokens, chunk), bf16),
            pltpu.VMEM((chunks, rows, tokens, chunk), bf16),
            pltpu.VMEM((chunks, rows, tokens, chunk), bf16),
            dma((7,)),
            dma((rows,)), dma((rows,)),
            dma((ycount, rows)), dma((ycount, rows)),
            dma((ycount, rows)), dma((ycount, rows)),
            dma((rows,)), dma((rows,)),
            dma((ycount,)), dma((ycount,)),
            dma((ycount,)), dma((ycount,)),
            dma((chunks,)), dma((chunks,)),
            dma((chunks, ycount)), dma((chunks, ycount)),
            dma((chunks, rows)), dma((chunks, rows)),
        ],
        compiler_params=pltpu.CompilerParams(collective_id=0, has_side_effects=True),
    )(
        cotangent[0], routes[0, 0], probs[0, 0],
        stash.reshape(columns, rows, tokens, 2 * units),
        w_gate[0, 0, 0], w_up[0, 0, 0], w_down[0, 0, 0],
    )
    return out[None]


def shifted_2(value, axis, steps):
    count = lax.axis_size(axis)
    pairs = [(source, (source + steps) % count) for source in range(count)]
    return lax.ppermute(value, axis, pairs)


def body(mesh, cotangent, routes, probs, stash, w_gate, w_up, w_down):
    if (
        mesh.shape["expert"] in (2, 4)
        and stash.shape[6] == cotangent.shape[1]
    ):
        return relay(mesh, cotangent, routes, probs, stash, w_gate, w_up, w_down)
    row_count = lax.axis_size("dp")
    column_count = lax.axis_size("expert")
    group_count = min(4, column_count)
    piece_count = column_count // group_count
    expert_count = group_count * row_count
    slot_most = stash.shape[6]
    model_width = w_gate.shape[4]
    piece_units = w_gate.shape[3]
    token_count = cotangent.shape[1]
    top_count = routes.shape[3]
    rows_dev = token_count * top_count
    code_count = expert_count * slot_most
    gate_piece = w_gate[0, 0, 0]
    up_piece = w_up[0, 0, 0]
    down_piece = w_down[0, 0, 0]
    earlier = lax.broadcasted_iota(jnp.int32, (rows_dev, rows_dev), 1) < lax.broadcasted_iota(
        jnp.int32, (rows_dev, rows_dev), 0
    )
    code_grid = lax.broadcasted_iota(jnp.int32, (rows_dev, code_count), 1)
    current = cotangent[0]
    shifted = shifted_2(current, "section", -1)
    expert_ids = routes[0, 0].reshape(-1)
    same_id = expert_ids[:, None] == expert_ids[None, :]
    ranked = jnp.sum(jnp.logical_and(same_id, earlier), axis=1)
    slot_code = expert_ids * slot_most + ranked
    selector = (slot_code[:, None] == code_grid).astype(jnp.bfloat16)
    grad_rows = (probs[0, 0][:, :, None] * shifted[:, None, :].astype(jnp.float32)).astype(
        jnp.bfloat16
    )
    grad_rows = grad_rows.reshape(rows_dev, model_width)
    packed = lax.dot_general(
        selector, grad_rows, (((0,), (0,)), ((), ())), preferred_element_type=jnp.float32
    )
    outgoing = packed.astype(jnp.bfloat16).reshape(group_count, row_count, slot_most, model_width)
    arrived = lax.all_to_all(outgoing, "dp", split_axis=1, concat_axis=1, tiled=True)
    copies = jnp.broadcast_to(
        arrived[:, None], (group_count, piece_count, row_count, slot_most, model_width)
    )
    copies = copies.reshape(column_count, row_count, slot_most, model_width)
    owned = lax.all_to_all(copies, "expert", split_axis=0, concat_axis=0, tiled=True)
    slot_rows = owned.reshape(-1, model_width)
    saved_pre = stash[0, 0, 0, 0].reshape(-1, 2 * piece_units)
    gate_pre = saved_pre[:, :piece_units].astype(jnp.float32)
    up_pre = saved_pre[:, piece_units:].astype(jnp.float32)
    grad_act = lax.dot_general(
        slot_rows, down_piece, (((1,), (1,)), ((), ())), preferred_element_type=jnp.float32
    )
    gate_sigmoid = jax.nn.sigmoid(gate_pre)
    grad_gate = (grad_act * up_pre * gate_sigmoid * (1.0 + gate_pre * (1.0 - gate_sigmoid))).astype(
        jnp.bfloat16
    )
    grad_up = (grad_act * gate_pre * gate_sigmoid).astype(jnp.bfloat16)
    partial_value = jnp.dot(grad_gate, gate_piece, preferred_element_type=jnp.float32)
    partial_value = (
        partial_value + jnp.dot(grad_up, up_piece, preferred_element_type=jnp.float32)
    ).astype(jnp.bfloat16)
    returned = lax.all_to_all(
        partial_value.reshape(column_count, row_count, slot_most, model_width),
        "expert",
        split_axis=0,
        concat_axis=0,
        tiled=True,
    )
    returned = returned.reshape(group_count, piece_count, row_count, slot_most, model_width)
    summed = jnp.sum(returned, axis=1, dtype=jnp.float32).astype(jnp.bfloat16)
    returned_rows = lax.all_to_all(summed, "dp", split_axis=1, concat_axis=1, tiled=True)
    token_select = jnp.sum(selector.reshape(token_count, top_count, code_count), axis=1)
    gathered = jnp.dot(
        token_select,
        returned_rows.reshape(code_count, model_width),
        preferred_element_type=jnp.float32,
    )
    current = (shifted.astype(jnp.float32) + gathered).astype(jnp.bfloat16)
    return current[None]


def solution(mesh):
    placed = (
        P("section", ("dp", "expert"), None),
        P("section", None, ("dp", "expert"), None),
        P("section", None, ("dp", "expert"), None),
        P("section", None, "dp", "expert", None, None, None, None),
        P("section", "dp", "expert", None, None),
        P("section", "dp", "expert", None, None),
        P("section", "dp", "expert", None, None),
    )
    return jax.shard_map(
        functools.partial(body, mesh),
        mesh=mesh,
        in_specs=placed,
        out_specs=P("section", ("dp", "expert"), None),
        check_vma=False,
    )
```

```python
import functools

import jax
import jax.numpy as jnp
from jax import lax
from jax.experimental import pallas as pl
from jax.experimental.pallas import tpu as pltpu
from jax.sharding import PartitionSpec as P

MESH = pl.DeviceIdType.MESH


def relay_kernel(
    sections, rows, columns, chunks,
    cot_hbm, routes_hbm, probs_hbm, stash, gate_hbm, up_hbm, down_hbm, out,
    cot, routes, probs, tok, wt, stash_v, gate_v, up_v, down_v, obuf, r1, s1, r2, s2, r3,
    load_sem, a_send, a_recv, y_send, y_recv, c_send, c_recv,
    wz_send, wz_recv, wy_send, wy_recv, wc_send, wc_recv,
    p1_send, p1_recv, p2_send, p2_recv, p3_send, p3_recv,
):
    sec = lax.axis_index("section")
    row = lax.axis_index("dp")
    col = lax.axis_index("expert")
    core = lax.rem(col, 2)
    ypos = col // 2
    ycount = columns // 2
    tokens, width = cot.shape
    units = down_v.shape[0]
    slots = columns * rows * tokens
    chunk = width // chunks
    mate = (sec, row, col + 1 - 2 * core)
    before = lax.rem(sec + sections - 1, sections)
    after = lax.rem(sec + 1, sections)

    def zpeer(k):
        return lax.rem(row + k, rows)

    def zfrom(k):
        return lax.rem(row + rows - k, rows)

    def ypeer(j):
        return lax.rem(col + 2 * j, columns)

    def yfrom(j):
        return lax.rem(col + columns - 2 * j, columns)

    def remote(src, dst, send, recv, device):
        return pltpu.make_async_remote_copy(
            src_ref=src, dst_ref=dst, send_sem=send, recv_sem=recv,
            device_id=device, device_id_type=MESH,
        )

    small = [
        pltpu.make_async_copy(cot_hbm, cot, load_sem.at[6]),
        pltpu.make_async_copy(routes_hbm, routes, load_sem.at[4]),
        pltpu.make_async_copy(probs_hbm, probs, load_sem.at[5]),
    ]
    loads = [
        pltpu.make_async_copy(stash, stash_v, load_sem.at[0]),
        pltpu.make_async_copy(down_hbm, down_v, load_sem.at[1]),
        pltpu.make_async_copy(gate_hbm, gate_v, load_sem.at[2]),
        pltpu.make_async_copy(up_hbm, up_v, load_sem.at[3]),
    ]

    for load in small:
        load.start()
    barrier = pltpu.get_barrier_semaphore()
    greeted = 0
    ring = [before] if sections == 2 else [before, after]
    for other in ring:
        for k in range(rows):
            pl.semaphore_signal(barrier, inc=1, device_id=(other, zpeer(k), col), device_id_type=MESH)
            greeted += 1
    for k in range(1, rows):
        pl.semaphore_signal(barrier, inc=1, device_id=(sec, zpeer(k), col), device_id_type=MESH)
        greeted += 1
    for j in range(1, ycount):
        pl.semaphore_signal(barrier, inc=1, device_id=(sec, row, ypeer(j)), device_id_type=MESH)
        greeted += 1
    pl.semaphore_signal(barrier, inc=1, device_id=mate, device_id_type=MESH)
    greeted += 1

    for load in loads:
        load.start()

    for load in small:
        load.wait()
    lanes = wt.shape[3]
    lane = lax.broadcasted_iota(jnp.int32, (tokens, lanes), 1)
    tile = jnp.zeros((tokens, lanes), jnp.float32)
    for k in range(routes.shape[1]):
        tile = tile + jnp.where(routes[:, k:k + 1] == lane, probs[:, k:k + 1], 0.0)
    wt[col, row] = tile

    pl.semaphore_wait(barrier, greeted)

    sends = []

    def go(copy):
        copy.start()
        sends.append(copy)

    def a_copy(k):
        return remote(cot, tok.at[col, row], a_send.at[k], a_recv.at[k], (before, zpeer(k), col))

    def a_wait(k):
        src = zfrom(k)
        remote(cot, tok.at[col, src], a_send.at[k], a_recv.at[k], mate).wait_recv()

    for k in range(rows - 1, -1, -1):
        go(a_copy(k))
    for k in range(rows - 1, 0, -1):
        go(remote(wt.at[col, row], wt.at[col, row], wz_send.at[k], wz_recv.at[k], (sec, zpeer(k), col)))

    for k in range(rows):
        a_wait(k)
        block = tok.at[col, zfrom(k)]
        for j in range(1, ycount):
            go(remote(block, block, y_send.at[j, k], y_recv.at[j, k], (sec, row, ypeer(j))))
        go(remote(block, block, c_send.at[0, k], c_recv.at[0, k], mate))
        if k == 0:
            for n in range(rows - 1, 0, -1):
                src = wt.at[col, zfrom(n)]
                remote(src, src, wz_send.at[n], wz_recv.at[n], mate).wait_recv()
            for j in range(1, ycount):
                go(remote(wt.at[col], wt.at[col], wy_send.at[j], wy_recv.at[j], (sec, row, ypeer(j))))
            go(remote(wt.at[col], wt.at[col], wc_send.at[0], wc_recv.at[0], mate))

    for j in range(1, ycount):
        part = wt.at[yfrom(j)]
        remote(part, part, wy_send.at[j], wy_recv.at[j], mate).wait_recv()
        go(remote(part, part, wc_send.at[j], wc_recv.at[j], mate))
    for k in range(rows - 1, -1, -1):
        for j in range(1, ycount):
            block = tok.at[yfrom(j), zfrom(k)]
            remote(block, block, y_send.at[j, k], y_recv.at[j, k], mate).wait_recv()
            go(remote(block, block, c_send.at[j, k], c_recv.at[j, k], mate))
    mate_col = col + 1 - 2 * core
    for j in range(ycount):
        part = wt.at[lax.rem(mate_col + columns - 2 * j, columns)]
        remote(part, part, wc_send.at[j], wc_recv.at[j], mate).wait_recv()

    expert = col * rows + row
    weights = wt[...].reshape(slots, lanes)
    wide = lax.broadcasted_iota(jnp.int32, (slots, lanes), 1)
    weight = jnp.sum(jnp.where(wide == expert, weights, 0.0), axis=1, keepdims=True)
    named = jnp.broadcast_to((weight > 0.0).astype(jnp.float32), (slots, slots))
    at_row = lax.broadcasted_iota(jnp.int32, (slots, slots), 0)
    at_col = lax.broadcasted_iota(jnp.int32, (slots, slots), 1)
    same = (at_row // tokens) == (at_col // tokens)
    lower = jnp.where(jnp.logical_and(same, at_col < at_row), 1.0, 0.0).astype(jnp.bfloat16)
    rank = jnp.dot(lower, named.astype(jnp.bfloat16), preferred_element_type=jnp.float32)
    spot = ((at_row // tokens) * tokens).astype(jnp.float32) + rank
    pick = jnp.where(at_col.astype(jnp.float32) == spot, named, 0.0).astype(jnp.bfloat16)
    loads[0].wait()
    saved = stash_v[...].astype(jnp.float32).reshape(slots, 2 * units).astype(jnp.bfloat16)
    saved = jnp.dot(pick, saved, preferred_element_type=jnp.float32)
    gate_pre = saved[:, :units]
    up_pre = saved[:, units:]
    sg = jax.nn.sigmoid(gate_pre)
    f_gate = up_pre * sg * (1.0 + gate_pre * (1.0 - sg))
    f_up = gate_pre * sg
    loads[1].wait()

    for k in range(rows - 1, -1, -1):
        for j in range(ycount):
            block = tok.at[lax.rem(mate_col + columns - 2 * j, columns), zfrom(k)]
            remote(block, block, c_send.at[j, k], c_recv.at[j, k], mate).wait_recv()

    moved = tok[...].astype(jnp.float32).reshape(slots, width)
    grad_rows = (moved * weight).astype(jnp.bfloat16)
    grad_act = lax.dot_general(
        grad_rows, down_v[...], (((1,), (1,)), ((), ())), preferred_element_type=jnp.float32
    )
    grad_gate = (grad_act * f_gate).astype(jnp.bfloat16)
    grad_up = (grad_act * f_up).astype(jnp.bfloat16)
    loads[2].wait()
    loads[3].wait()

    def p1(t):
        return remote(obuf.at[t, 1 - core], r1.at[t], p1_send.at[t], p1_recv.at[t], mate)

    def p2(t, j):
        return remote(s1.at[t, j], r2.at[t, j], p2_send.at[t, j], p2_recv.at[t, j], (sec, row, ypeer(j)))

    def p3(t, k):
        return remote(s2.at[t, k], r3.at[t, k], p3_send.at[t, k], p3_recv.at[t, k], (sec, zpeer(k), col))

    def f32(value):
        return value.astype(jnp.float32)

    for t in range(chunks):
        span = slice(t * chunk, (t + 1) * chunk)
        part = jnp.dot(grad_gate, gate_v[:, span], preferred_element_type=jnp.float32)
        part = part + jnp.dot(grad_up, up_v[:, span], preferred_element_type=jnp.float32)
        part = part.reshape(ycount, 2, rows, tokens, chunk).astype(jnp.bfloat16)
        obuf[t, 0] = part[:, 0]
        obuf[t, 1] = part[:, 1]
        go(p1(t))
    for t in range(chunks):
        p1(t).wait_recv()
        for j in range(1, ycount):
            y = lax.rem(ypos + j, ycount)
            s1[t, j] = (f32(obuf[t, core, y]) + f32(r1[t, y])).astype(jnp.bfloat16)
            go(p2(t, j))
    for t in range(chunks):
        for j in range(1, ycount):
            p2(t, j).wait_recv()
        for k in range(1, rows):
            to = zpeer(k)
            total = f32(obuf[t, core, ypos, to]) + f32(r1[t, ypos, to])
            for j in range(1, ycount):
                total = total + f32(r2[t, j, to])
            s2[t, k] = total.astype(jnp.bfloat16)
            go(p3(t, k))
    for t in range(chunks):
        span = slice(t * chunk, (t + 1) * chunk)
        total = f32(obuf[t, core, ypos, row]) + f32(r1[t, ypos, row])
        for j in range(1, ycount):
            total = total + f32(r2[t, j, row])
        for k in range(1, rows):
            p3(t, k).wait_recv()
            total = total + f32(r3[t, k])
        out[:, span] = (f32(tok[col, row, :, span]) + total).astype(jnp.bfloat16)
    for copy in sends:
        copy.wait_send()


def relay(mesh, cotangent, routes, probs, stash, w_gate, w_up, w_down):
    sections, rows, columns = (mesh.shape[name] for name in ("section", "dp", "expert"))
    tokens, width = cotangent.shape[1:]
    units = w_gate.shape[3]
    ycount = columns // 2
    lanes = -(-rows * columns // 128) * 128
    chunks = max(width // 1024, 1)
    chunk = width // chunks
    bf16 = jnp.bfloat16
    dma = pltpu.SemaphoreType.DMA
    vmem = pl.BlockSpec(memory_space=pltpu.VMEM)
    hbm = pl.BlockSpec(memory_space=pl.ANY)
    out = pl.pallas_call(
        functools.partial(relay_kernel, sections, rows, columns, chunks),
        out_shape=pltpu.VMEM((tokens, width), bf16),
        in_specs=[hbm, hbm, hbm, hbm, hbm, hbm, hbm],
        out_specs=vmem,
        scratch_shapes=[
            pltpu.VMEM((tokens, width), bf16),
            pltpu.VMEM(routes.shape[2:], jnp.int32),
            pltpu.VMEM(probs.shape[2:], jnp.float32),
            pltpu.VMEM((columns, rows, tokens, width), bf16),
            pltpu.VMEM((columns, rows, tokens, lanes), jnp.float32),
            pltpu.VMEM((columns, rows, tokens, 2 * units), bf16),
            pltpu.VMEM((units, width), bf16),
            pltpu.VMEM((units, width), bf16),
            pltpu.VMEM((units, width), bf16),
            pltpu.VMEM((chunks, 2, ycount, rows, tokens, chunk), bf16),
            pltpu.VMEM((chunks, ycount, rows, tokens, chunk), bf16),
            pltpu.VMEM((chunks, ycount, rows, tokens, chunk), bf16),
            pltpu.VMEM((chunks, ycount, rows, tokens, chunk), bf16),
            pltpu.VMEM((chunks, rows, tokens, chunk), bf16),
            pltpu.VMEM((chunks, rows, tokens, chunk), bf16),
            dma((7,)),
            dma((rows,)), dma((rows,)),
            dma((ycount, rows)), dma((ycount, rows)),
            dma((ycount, rows)), dma((ycount, rows)),
            dma((rows,)), dma((rows,)),
            dma((ycount,)), dma((ycount,)),
            dma((ycount,)), dma((ycount,)),
            dma((chunks,)), dma((chunks,)),
            dma((chunks, ycount)), dma((chunks, ycount)),
            dma((chunks, rows)), dma((chunks, rows)),
        ],
        compiler_params=pltpu.CompilerParams(collective_id=0, has_side_effects=True),
    )(
        cotangent[0], routes[0, 0], probs[0, 0],
        stash.reshape(columns, rows, tokens, 2 * units),
        w_gate[0, 0, 0], w_up[0, 0, 0], w_down[0, 0, 0],
    )
    return out[None]


def shifted_2(value, axis, steps):
    count = lax.axis_size(axis)
    pairs = [(source, (source + steps) % count) for source in range(count)]
    return lax.ppermute(value, axis, pairs)


def body(mesh, cotangent, routes, probs, stash, w_gate, w_up, w_down):
    if (
        mesh.shape["expert"] in (2, 4)
        and stash.shape[6] == cotangent.shape[1]
    ):
        return relay(mesh, cotangent, routes, probs, stash, w_gate, w_up, w_down)
    row_count = lax.axis_size("dp")
    column_count = lax.axis_size("expert")
    group_count = min(4, column_count)
    piece_count = column_count // group_count
    expert_count = group_count * row_count
    slot_most = stash.shape[6]
    model_width = w_gate.shape[4]
    piece_units = w_gate.shape[3]
    token_count = cotangent.shape[1]
    top_count = routes.shape[3]
    rows_dev = token_count * top_count
    code_count = expert_count * slot_most
    gate_piece = w_gate[0, 0, 0]
    up_piece = w_up[0, 0, 0]
    down_piece = w_down[0, 0, 0]
    earlier = lax.broadcasted_iota(jnp.int32, (rows_dev, rows_dev), 1) < lax.broadcasted_iota(
        jnp.int32, (rows_dev, rows_dev), 0
    )
    code_grid = lax.broadcasted_iota(jnp.int32, (rows_dev, code_count), 1)
    current = cotangent[0]
    shifted = shifted_2(current, "section", -1)
    expert_ids = routes[0, 0].reshape(-1)
    same_id = expert_ids[:, None] == expert_ids[None, :]
    ranked = jnp.sum(jnp.logical_and(same_id, earlier), axis=1)
    slot_code = expert_ids * slot_most + ranked
    selector = (slot_code[:, None] == code_grid).astype(jnp.bfloat16)
    grad_rows = (probs[0, 0][:, :, None] * shifted[:, None, :].astype(jnp.float32)).astype(
        jnp.bfloat16
    )
    grad_rows = grad_rows.reshape(rows_dev, model_width)
    packed = lax.dot_general(
        selector, grad_rows, (((0,), (0,)), ((), ())), preferred_element_type=jnp.float32
    )
    outgoing = packed.astype(jnp.bfloat16).reshape(group_count, row_count, slot_most, model_width)
    arrived = lax.all_to_all(outgoing, "dp", split_axis=1, concat_axis=1, tiled=True)
    copies = jnp.broadcast_to(
        arrived[:, None], (group_count, piece_count, row_count, slot_most, model_width)
    )
    copies = copies.reshape(column_count, row_count, slot_most, model_width)
    owned = lax.all_to_all(copies, "expert", split_axis=0, concat_axis=0, tiled=True)
    slot_rows = owned.reshape(-1, model_width)
    saved_pre = stash[0, 0, 0, 0].reshape(-1, 2 * piece_units)
    gate_pre = saved_pre[:, :piece_units].astype(jnp.float32)
    up_pre = saved_pre[:, piece_units:].astype(jnp.float32)
    grad_act = lax.dot_general(
        slot_rows, down_piece, (((1,), (1,)), ((), ())), preferred_element_type=jnp.float32
    )
    gate_sigmoid = jax.nn.sigmoid(gate_pre)
    grad_gate = (grad_act * up_pre * gate_sigmoid * (1.0 + gate_pre * (1.0 - gate_sigmoid))).astype(
        jnp.bfloat16
    )
    grad_up = (grad_act * gate_pre * gate_sigmoid).astype(jnp.bfloat16)
    partial_value = jnp.dot(grad_gate, gate_piece, preferred_element_type=jnp.float32)
    partial_value = (
        partial_value + jnp.dot(grad_up, up_piece, preferred_element_type=jnp.float32)
    ).astype(jnp.bfloat16)
    returned = lax.all_to_all(
        partial_value.reshape(column_count, row_count, slot_most, model_width),
        "expert",
        split_axis=0,
        concat_axis=0,
        tiled=True,
    )
    returned = returned.reshape(group_count, piece_count, row_count, slot_most, model_width)
    summed = jnp.sum(returned, axis=1, dtype=jnp.float32).astype(jnp.bfloat16)
    returned_rows = lax.all_to_all(summed, "dp", split_axis=1, concat_axis=1, tiled=True)
    token_select = jnp.sum(selector.reshape(token_count, top_count, code_count), axis=1)
    gathered = jnp.dot(
        token_select,
        returned_rows.reshape(code_count, model_width),
        preferred_element_type=jnp.float32,
    )
    current = (shifted.astype(jnp.float32) + gathered).astype(jnp.bfloat16)
    return current[None]


def solution(mesh):
    placed = (
        P("section", ("dp", "expert"), None),
        P("section", None, ("dp", "expert"), None),
        P("section", None, ("dp", "expert"), None),
        P("section", None, "dp", "expert", None, None, None, None),
        P("section", "dp", "expert", None, None),
        P("section", "dp", "expert", None, None),
        P("section", "dp", "expert", None, None),
    )
    return jax.shard_map(
        functools.partial(body, mesh),
        mesh=mesh,
        in_specs=placed,
        out_specs=P("section", ("dp", "expert"), None),
        check_vma=False,
    )
```
